32 devices in a mesh: dp: 8 (over z, x), tensor: 4 (over y, core).
Axes of the slice: x: 2, y: 2, z: 4, core: 2. Of those that a mesh axis runs over, the one named last changes fastest.
Arguments:
- hidden_in: bfloat16 [4096, 2048], P(('dp', 'tensor')), may hold values from -30 to 30
- segment_ids: int32 [8, 512], P('dp'), may hold values from 0 to 3, as said below
- query_weight: bfloat16 [2048, 2048], P('dp', 'tensor'), may hold values from -1 to 1
- key_weight: bfloat16 [2048, 2048], P('dp', 'tensor'), may hold values from -1 to 1
- value_weight: bfloat16 [2048, 2048], P('dp', 'tensor'), may hold values from -0.125 to 0.125
- output_weight: bfloat16 [2048, 2048], P('tensor', 'dp'), may hold values from -1 to 1
- gate_weight: bfloat16 [2048, 8192], P('dp', 'tensor'), may hold values from -0.125 to 0.125
- up_weight: bfloat16 [2048, 8192], P('dp', 'tensor'), may hold values from -0.125 to 0.125
- down_weight: bfloat16 [8192, 2048], P('tensor', 'dp'), may hold values from -1 to 1
- query_gain: float32 [2048], P(('dp', 'tensor')), may hold values from 0.5 to 1.5
- key_gain: float32 [2048], P(('dp', 'tensor')), may hold values from 0.5 to 1.5
- attention_gain: float32 [2048], P(('dp', 'tensor')), may hold values from 0.5 to 1.5
- feedforward_gain: float32 [2048], P(('dp', 'tensor')), may hold values from 0.5 to 1.5
- out_grad: bfloat16 [4096, 2048], P(('dp', 'tensor')), may hold values from -6 to 6
Outputs:
- hidden_out: bfloat16 [4096, 2048], P(('dp', 'tensor'))
- grad_in: float32 [4096, 2048], P(('dp', 'tensor'))
- grad_query_weight: float32 [2048, 2048], P('dp', 'tensor')
- grad_key_weight: float32 [2048, 2048], P('dp', 'tensor')
- grad_value_weight: float32 [2048, 2048], P('dp', 'tensor')
- grad_output_weight: float32 [2048, 2048], P('tensor', 'dp')
- grad_gate_weight: float32 [2048, 8192], P('dp', 'tensor')
- grad_up_weight: float32 [2048, 8192], P('dp', 'tensor')
- grad_down_weight: float32 [8192, 2048], P('tensor', 'dp')
- grad_query_gain: float32 [2048], P(('dp', 'tensor'))
- grad_key_gain: float32 [2048], P(('dp', 'tensor'))
- grad_attention_gain: float32 [2048], P(('dp', 'tensor'))
- grad_feedforward_gain: float32 [2048], P(('dp', 'tensor'))
The draws below stay inside these ranges and needn't reach their ends.
Inputs may be any that keep to these rules, and one draw needn't show every extreme that they name: `segment_ids`: segment numbers count the documents of each sequence from 0 and never fall along it; every sequence holds exactly 4 documents, each of 50 tokens or more.
All inputs are finite; a program needn't handle non-finite values.
Results may differ from the reference program's by a relative error of at most 0.019.
Values may be sent and summed in bfloat16 or wider, within the bound.
No kernel may reach another device: no remote copies, remote signals or barrier semaphores. Data moves between devices by JAX's collectives and lax.ppermute only.
A program may use at most 192 MiB of HBM per device.

```python
import jax
import jax.numpy as jnp
from jax import lax

D = 2048
HEADS = 16
HEAD_DIM = 128
FF = 8192
SEQ_LEN = 512
DOC_MIN = 50
DOCS = 4
SEQS = 1
TOK_DEV = 512
TOKENS = 4096
SEQ_ALL = 8
N_DP = 8


def column_scaled(seed_key, row_total, column_total, factor):
    first_key, second_key = jax.random.split(seed_key)
    entries = jnp.clip(jax.random.normal(first_key, (row_total, column_total), jnp.float32), -5.0, 5.0)
    column = jnp.exp(jax.random.uniform(second_key, (column_total,), jnp.float32, -1.15, 1.15))
    return entries * column[None, :] * factor


def draw_hidden_in(key, part):
    seed_key = jax.random.fold_in(key, 101)
    first_key, second_key = jax.random.split(seed_key)
    row_scale = jnp.exp(jax.random.uniform(second_key, (TOKENS,), jnp.float32, -1.15, 1.15))
    return (column_scaled(first_key, TOKENS, D, 0.6) * row_scale[:, None]).astype(jnp.bfloat16)


def draw_segment_ids(key, part):
    seed_key = jax.random.fold_in(key, 606)
    spare = SEQ_LEN - DOCS * DOC_MIN
    cuts = jnp.sort(jax.random.randint(seed_key, (SEQ_ALL, DOCS - 1), 0, spare + 1, dtype=jnp.int32), axis=1)
    starts = cuts + DOC_MIN * jnp.arange(1, DOCS, dtype=jnp.int32)[None, :]
    places = jnp.arange(SEQ_LEN, dtype=jnp.int32)
    return jnp.sum((places[None, :, None] >= starts[:, None, :]).astype(jnp.int32), axis=2).astype(jnp.int32)


def draw_query_weight(key, part):
    return column_scaled(jax.random.fold_in(key, 202), D, D, 0.6 * D ** (-0.5)).astype(jnp.bfloat16)


def draw_key_weight(key, part):
    return column_scaled(jax.random.fold_in(key, 303), D, D, 0.6 * D ** (-0.5)).astype(jnp.bfloat16)


def draw_output_weight(key, part):
    return column_scaled(jax.random.fold_in(key, 404), D, D, 0.6 * D ** (-0.5)).astype(jnp.bfloat16)


def draw_down_weight(key, part):
    return column_scaled(jax.random.fold_in(key, 505), FF, D, 0.6 * FF ** (-0.5)).astype(jnp.bfloat16)


def raised(values, own_key, source, target, parts, factor):
    def block_of(position):
        return (jnp.arange(values.shape[position]) // (values.shape[position] // parts)).reshape((-1,) + (1,) * (values.ndim - 1 - position))

    one_side = jax.random.permutation(own_key, parts)[block_of(target)]
    far = (block_of(target) + parts // 2) % parts
    return jnp.where((block_of(source) == one_side) | (block_of(source) == far), factor * values, values)


def block_levels(own_key, extent, cuts, least, largest):
    loudness, own = 1.0, jax.random.fold_in(own_key, 6)
    for position, blocks in cuts:
        steps = jnp.exp(jax.random.uniform(jax.random.fold_in(own, position), (blocks,), jnp.float32, least / len(cuts), largest / len(cuts)))
        loudness = loudness * jnp.repeat(steps, extent[position] // blocks).reshape([-1 if axis == position else 1 for axis in range(len(extent))])
    return loudness


def scatter_about(own_key, extent, deviation, bound, cuts=(), held_as=jnp.bfloat16):
    values = jax.random.normal(own_key, extent, jnp.float32) * deviation
    if len(cuts) > 0:
        values = block_levels(own_key, extent, cuts, -0.22, 0.18) * values
    return jnp.clip(values, min=-bound, max=bound).astype(held_as)


def noise_with(stream_key, extent, scale, limit, pieces, heavy, held_as=jnp.bfloat16):
    array = scale * jax.random.normal(stream_key, extent, jnp.float32)
    if pieces:
        array = array * block_levels(stream_key, extent, pieces, -0.22, 0.18)
    return jnp.clip(raised(array, jax.random.fold_in(stream_key, 3), *heavy), -limit, limit).astype(held_as)


def setup_inputs(seed: int = 0) -> dict:
    arg_keys = jax.random.split(jax.random.key(seed), 15)
    hidden_in = draw_hidden_in(jax.random.fold_in(arg_keys[14], 71), 0)
    segment_ids = draw_segment_ids(jax.random.fold_in(arg_keys[14], 71), 0)
    query_weight = draw_query_weight(jax.random.fold_in(arg_keys[14], 71), 0)
    key_weight = draw_key_weight(jax.random.fold_in(arg_keys[14], 71), 0)
    value_weight = scatter_about(arg_keys[4], (D, D), D ** -0.5, 0.125, ((0, 8), (1, 4)))
    output_weight = draw_output_weight(jax.random.fold_in(arg_keys[14], 71), 0)
    gate_weight = scatter_about(arg_keys[6], (D, FF), D ** -0.5, 0.125, ((0, 8), (1, 4)))
    up_weight = scatter_about(arg_keys[7], (D, FF), D ** -0.5, 0.125, ((0, 8), (1, 4)))
    down_weight = draw_down_weight(jax.random.fold_in(arg_keys[14], 71), 0)
    query_gain = jnp.clip(1.0 + 0.1 * jax.random.normal(arg_keys[9], (D,), jnp.float32), 0.5, 1.5)
    key_gain = jnp.clip(1.0 + 0.1 * jax.random.normal(arg_keys[10], (D,), jnp.float32), 0.5, 1.5)
    attention_gain = jnp.clip(1.0 + 0.1 * jax.random.normal(arg_keys[11], (D,), jnp.float32), 0.5, 1.5)
    feedforward_gain = jnp.clip(1.0 + 0.1 * jax.random.normal(arg_keys[12], (D,), jnp.float32), 0.5, 1.5)
    out_grad = noise_with(arg_keys[13], (TOKENS, D), 1.0, 6.0, ((0, 32),), (0, 1, 32, 2.75))
    return dict(hidden_in=hidden_in, segment_ids=segment_ids, query_weight=query_weight, key_weight=key_weight, value_weight=value_weight, output_weight=output_weight, gate_weight=gate_weight, up_weight=up_weight, down_weight=down_weight, query_gain=query_gain, key_gain=key_gain, attention_gain=attention_gain, feedforward_gain=feedforward_gain, out_grad=out_grad)


epsilon = 1e-06
rotary_base = 500000.0

def rotate_half(values):
    midpoint = values.shape[-1] // 2
    return jnp.concatenate([-values[..., midpoint:], values[..., :midpoint]], axis=-1)

def rotary_tables(segment_rows):
    seq_length = segment_rows.shape[1]
    earlier = (segment_rows[:, None, :] < segment_rows[:, :, None]).astype(jnp.int32)
    starts = lax.optimization_barrier(jnp.sum(earlier, axis=2, dtype=jnp.int32))
    positions = jnp.arange(seq_length, dtype=jnp.int32)[None, :] - starts
    inverse = rotary_base ** (-(jnp.arange(HEAD_DIM // 2, dtype=jnp.float32) * 2.0) / HEAD_DIM)
    angles = positions.astype(jnp.float32)[:, :, None] * inverse[None, None, :]
    angles = jnp.concatenate([angles, angles], axis=-1)
    return (jnp.cos(angles), jnp.sin(angles))

def attention_mask(segment_rows):
    seq_length = segment_rows.shape[1]
    same_doc = segment_rows[:, :, None] == segment_rows[:, None, :]
    indices = jnp.arange(seq_length, dtype=jnp.int32)
    causal = indices[:, None] >= indices[None, :]
    return jnp.logical_and(same_doc, causal[None, :, :])[:, None, :, :]

def apply_rotary(values, cosine_table, sine_table):
    return values * cosine_table[:, :, None, :] + rotate_half(values) * sine_table[:, :, None, :]

def rotary_back(gradient, cosine_table, sine_table):
    return gradient * cosine_table[:, :, None, :] - rotate_half(gradient * sine_table[:, :, None, :])

def rms_inverse(values):
    return lax.rsqrt(lax.optimization_barrier(jnp.mean(values * values, axis=1)) + epsilon)

def norm_back(inputs, inverse, weighted, mean_term):
    return inverse[:, None] * weighted - inputs * (inverse ** 3)[:, None] * mean_term[:, None]

def matmul(former, latter):
    return jnp.dot(former, latter, preferred_element_type=jnp.float32)

def reference(hidden_in, segment_ids, query_weight, key_weight, value_weight, output_weight, gate_weight, up_weight, down_weight, query_gain, key_gain, attention_gain, feedforward_gain, out_grad):
    scale_factor = HEAD_DIM ** (-0.5)
    split_shape = (SEQS, SEQ_LEN, HEADS, HEAD_DIM)
    grouped_in = hidden_in.reshape(N_DP, TOK_DEV, D)
    grouped_segments = segment_ids.reshape(N_DP, SEQS, SEQ_LEN)
    grouped_grad = out_grad.reshape(N_DP, TOK_DEV, D)

    def group_step(carry, group):
        tokens, segment_rows, grad_rows = group
        cosine_table, sine_table = rotary_tables(segment_rows)
        allowed = attention_mask(segment_rows)
        query_raw = matmul(tokens, query_weight)
        key_raw = matmul(tokens, key_weight)
        value_raw = matmul(tokens, value_weight)
        query_inv = rms_inverse(query_raw)
        key_inv = rms_inverse(key_raw)
        query_rot = apply_rotary((query_raw * query_inv[:, None] * query_gain).reshape(split_shape), cosine_table, sine_table).astype(jnp.bfloat16)
        key_rot = apply_rotary((key_raw * key_inv[:, None] * key_gain).reshape(split_shape), cosine_table, sine_table).astype(jnp.bfloat16)
        value_cast = value_raw.astype(jnp.bfloat16).reshape(split_shape)
        scores = jnp.einsum('sqhd,skhd->shqk', query_rot.astype(jnp.float32), key_rot.astype(jnp.float32)) * scale_factor
        log_totals = jnp.log(lax.optimization_barrier(jnp.sum(jnp.where(allowed, jnp.exp(scores), 0.0), axis=-1)))
        soft_weights = jnp.where(allowed, jnp.exp(scores - log_totals[..., None]), 0.0)
        soft_cast = soft_weights.astype(jnp.bfloat16)
        context = jnp.einsum('shqk,skhd->sqhd', soft_cast.astype(jnp.float32), value_cast.astype(jnp.float32)).astype(jnp.bfloat16).reshape(TOK_DEV, D)
        attention_sum = matmul(context, output_weight)
        attention_inv = rms_inverse(attention_sum)
        residual = tokens.astype(jnp.float32) + attention_sum * attention_inv[:, None] * attention_gain
        residual_cast = residual.astype(jnp.bfloat16)
        gate_pre = matmul(residual_cast, gate_weight)
        up_pre = matmul(residual_cast, up_weight)
        sigmoid_gate = jax.nn.sigmoid(gate_pre)
        activated = gate_pre * sigmoid_gate
        hidden_units = (activated * up_pre).astype(jnp.bfloat16)
        feed_sum = matmul(hidden_units, down_weight)
        feed_inv = rms_inverse(feed_sum)
        group_out = (residual + feed_sum * feed_inv[:, None] * feedforward_gain).astype(jnp.bfloat16)
        upstream = grad_rows.astype(jnp.float32)
        weighted = feedforward_gain * upstream
        feed_gain_grad = lax.optimization_barrier(jnp.sum(upstream * feed_sum * feed_inv[:, None], axis=0))
        feed_grad = norm_back(feed_sum, feed_inv, weighted, lax.optimization_barrier(jnp.mean(weighted * feed_sum, axis=1))).astype(jnp.bfloat16)
        hidden_grad = matmul(feed_grad, down_weight.T)
        down_weight_grad = matmul(hidden_units.T, feed_grad)
        gate_grad = (hidden_grad * up_pre * sigmoid_gate * (1.0 + gate_pre * (1.0 - sigmoid_gate))).astype(jnp.bfloat16)
        up_grad = (hidden_grad * activated).astype(jnp.bfloat16)
        gate_weight_grad = matmul(residual_cast.T, gate_grad)
        up_weight_grad = matmul(residual_cast.T, up_grad)
        stream_grad = upstream + matmul(gate_grad, gate_weight.T) + matmul(up_grad, up_weight.T)
        attention_weighted = attention_gain * stream_grad
        attention_gain_grad = lax.optimization_barrier(jnp.sum(stream_grad * attention_sum * attention_inv[:, None], axis=0))
        attention_grad = norm_back(attention_sum, attention_inv, attention_weighted, lax.optimization_barrier(jnp.mean(attention_weighted * attention_sum, axis=1))).astype(jnp.bfloat16)
        output_weight_grad = matmul(context.T, attention_grad)
        context_grad = matmul(attention_grad, output_weight.T).astype(jnp.bfloat16).reshape(split_shape)
        value_grad = jnp.einsum('shqk,sqhd->skhd', soft_cast.astype(jnp.float32), context_grad.astype(jnp.float32)).astype(jnp.bfloat16).reshape(TOK_DEV, D)
        soft_grad = jnp.einsum('sqhd,skhd->shqk', context_grad.astype(jnp.float32), value_cast.astype(jnp.float32))
        row_inner = lax.optimization_barrier(jnp.sum(soft_weights * soft_grad, axis=-1))
        score_grad = (soft_weights * (soft_grad - row_inner[..., None]) * scale_factor).astype(jnp.bfloat16)
        query_rot_grad = jnp.einsum('shqk,skhd->sqhd', score_grad.astype(jnp.float32), key_rot.astype(jnp.float32))
        key_rot_grad = jnp.einsum('shqk,sqhd->skhd', score_grad.astype(jnp.float32), query_rot.astype(jnp.float32))
        query_norm_grad = rotary_back(query_rot_grad, cosine_table, sine_table).reshape(TOK_DEV, D)
        key_norm_grad = rotary_back(key_rot_grad, cosine_table, sine_table).reshape(TOK_DEV, D)
        query_gain_grad = lax.optimization_barrier(jnp.sum(query_norm_grad * query_raw * query_inv[:, None], axis=0))
        key_gain_grad = lax.optimization_barrier(jnp.sum(key_norm_grad * key_raw * key_inv[:, None], axis=0))
        query_weighted = query_gain * query_norm_grad
        key_weighted = key_gain * key_norm_grad
        query_grad = norm_back(query_raw, query_inv, query_weighted, lax.optimization_barrier(jnp.mean(query_weighted * query_raw, axis=1))).astype(jnp.bfloat16)
        key_grad = norm_back(key_raw, key_inv, key_weighted, lax.optimization_barrier(jnp.mean(key_weighted * key_raw, axis=1))).astype(jnp.bfloat16)
        group_grad_in = stream_grad + matmul(query_grad, query_weight.T) + matmul(key_grad, key_weight.T) + matmul(value_grad, value_weight.T)
        additions = (matmul(tokens.T, query_grad), matmul(tokens.T, key_grad), matmul(tokens.T, value_grad), output_weight_grad, gate_weight_grad, up_weight_grad, down_weight_grad, query_gain_grad, key_gain_grad, attention_gain_grad, feed_gain_grad)
        new_carry = tuple((former + latter for former, latter in zip(carry, additions)))
        return (new_carry, (group_out, group_grad_in))
    initial = (jnp.zeros((D, D), jnp.float32), jnp.zeros((D, D), jnp.float32), jnp.zeros((D, D), jnp.float32), jnp.zeros((D, D), jnp.float32), jnp.zeros((D, FF), jnp.float32), jnp.zeros((D, FF), jnp.float32), jnp.zeros((FF, D), jnp.float32), jnp.zeros((D,), jnp.float32), jnp.zeros((D,), jnp.float32), jnp.zeros((D,), jnp.float32), jnp.zeros((D,), jnp.float32))
    totals, (outputs, inputs_grad) = lax.scan(group_step, initial, (grouped_in, grouped_segments, grouped_grad))
    return (outputs.reshape(TOKENS, D), inputs_grad.reshape(TOKENS, D), totals[0], totals[1], totals[2], totals[3], totals[4], totals[5], totals[6], totals[7], totals[8], totals[9], totals[10])
```

```python
import math

import jax
import jax.numpy as jnp
from jax import lax
from jax.sharding import Mesh
from jax.sharding import PartitionSpec as P

HEAD_DIM = 128

epsilon = 1e-06
rotary_base = 500000.0


def swap(values, axis):
    return lax.ppermute(values, axis, [(0, 1), (1, 0)])


def narrow(values):
    return values.astype(jnp.bfloat16)


def wide(values):
    return values.astype(jnp.float32)


def dot(former, latter, former_dim, latter_dim):
    return lax.dot_general(
        former,
        latter,
        (((former_dim,), (latter_dim,)), ((), ())),
        preferred_element_type=jnp.float32,
    )


def rotate_half(values):
    midpoint = values.shape[-1] // 2
    return jnp.concatenate([-values[..., midpoint:], values[..., :midpoint]], axis=-1)


def rms_inverse(values):
    return lax.rsqrt(jnp.mean(values * values, axis=1) + epsilon)


def norm_back(inputs, inverse, weighted, mean_term):
    return inverse[:, None] * weighted - inputs * (inverse**3)[:, None] * mean_term[:, None]


def make_body(dp_axes, tp_axes):
    high, pair = dp_axes[0], dp_axes[1]
    lows = dp_axes[2:]
    row_axes = (high,) + lows
    far, near = tp_axes

    def on(axis):
        return lax.axis_index(axis) == 1

    def flip_if(axis, values, dim):
        return jnp.where(on(axis), jnp.flip(values, dim), values)

    def in_order(axis, mine, theirs, dim):
        first = jnp.where(on(axis), theirs, mine)
        second = jnp.where(on(axis), mine, theirs)
        return jnp.concatenate([first, second], axis=dim)

    def halves(axis, values, dim):
        lower, upper = jnp.split(values, 2, axis=dim)
        return jnp.where(on(axis), upper, lower), jnp.where(on(axis), lower, upper)

    bits = len(dp_axes)

    def to_relative(values):
        lead = values.shape[:-1]
        k = len(lead)
        values = values.reshape(lead + (2,) * bits + (-1,))
        for i, axis in enumerate(dp_axes):
            if axis != pair:
                values = flip_if(axis, values, k + i)
        order = [k + i for i in range(bits - 1, 1, -1)] + [k, k + 1, k + bits]
        return values.transpose(tuple(range(k)) + tuple(order)).reshape(lead + (-1,))

    def from_relative(values):
        lead = values.shape[:-1]
        k = len(lead)
        values = values.reshape(lead + (2,) * bits + (-1,))
        order = [k + bits - 2, k + bits - 1] + [k + i for i in range(bits - 3, -1, -1)] + [k + bits]
        values = values.transpose(tuple(range(k)) + tuple(order))
        for i, axis in enumerate(dp_axes):
            if axis != pair:
                values = flip_if(axis, values, k + i)
        return values.reshape(lead + (-1,))

    def gather_weight(shards):
        mine, theirs = zip(*[halves(pair, shard, 1) for shard in shards])
        mine, theirs = jnp.concatenate(mine, axis=1), jnp.concatenate(theirs, axis=1)
        pieces = [in_order(pair, mine, swap(theirs, pair), 0)]
        for axis in row_axes:
            pieces = pieces + [swap(piece, axis) for piece in pieces]
        return jnp.concatenate(pieces, axis=0)

    def scatter_weight(inputs, gradient, widths):
        half = inputs.shape[1] // 2
        arrived = swap(narrow(dot(inputs[:, half:], gradient, 0, 0)), lows[-1])
        total = dot(inputs[:, :half], gradient, 0, 0) + wide(arrived)
        for axis in lows[-2::-1] + (high,):
            half = total.shape[0] // 2
            total = total[:half] + wide(swap(narrow(total[half:]), axis))
        mine, theirs = halves(pair, total, 0)
        theirs = wide(swap(narrow(theirs), pair))
        results, start = [], 0
        for width in widths:
            results.append(
                in_order(pair, mine[:, start : start + width], theirs[:, start : start + width], 1)
            )
            start += width
        return results

    def gather_tokens(values):
        half = values.shape[1] // 2
        left, right = values[:, :half], values[:, half:]
        left = jnp.stack([left, swap(left, far)])
        right = jnp.stack([right, swap(right, pair)])
        left = jnp.stack([left, swap(left, pair)])
        right = jnp.stack([right, swap(right, far)], axis=1)
        both = jnp.concatenate([left, right], axis=-1)
        both = jnp.stack([both, swap(both, near)], axis=1)
        return both.reshape(-1, values.shape[1])

    def scatter_tokens(former, latter):
        former = former.reshape(2, 2, -1, former.shape[1])
        tokens = former.shape[2] // 2
        model = latter.shape[0]
        half = model // 2

        def product(part):
            return dot(part.reshape(-1, part.shape[-1]), latter, 1, 1)

        arrived = swap(narrow(product(former[:, 1])), near)
        total = (product(former[:, 0]) + wide(arrived)).reshape(2, 2, tokens, model)
        left, right = total[..., :half], total[..., half:]
        left = left[:, 0] + wide(swap(narrow(left[:, 1]), far))
        right = right[0] + wide(swap(narrow(right[1]), pair))
        left = left[0] + wide(swap(narrow(left[1]), pair))
        right = right[0] + wide(swap(narrow(right[1]), far))
        return jnp.concatenate([left, right], axis=-1)

    def sum_group(values):
        shape = values.shape
        values = values.reshape(shape[:-1] + (2, 2, 2, -1))
        k = len(shape) - 1
        for axis, dim in ((near, k + 1), (far, k + 2), (pair, k)):
            values = values + jnp.flip(swap(values, axis), dim)
        return values.reshape(shape)

    def gather_gains(gains):
        values = jnp.stack(gains)
        for axis in (near, far, pair):
            values = in_order(axis, values, swap(values, axis), 1)
        for axis in row_axes:
            values = jnp.concatenate([values, swap(values, axis)], axis=1)
        return values

    def scatter_gains(values):
        for axis in lows[::-1] + (high,):
            kept, sent = jnp.split(values, 2, axis=1)
            values = kept + swap(sent, axis)
        for axis in (pair, far, near):
            kept, sent = halves(axis, values, 1)
            values = kept + swap(sent, axis)
        return values

    def token_tables(segment_row):
        seq_length = segment_row.shape[1]
        rows = jnp.concatenate([segment_row, swap(segment_row, pair)], axis=0)
        earlier = (rows[:, None, :] < rows[:, :, None]).astype(jnp.int32)
        starts = jnp.sum(earlier, axis=2, dtype=jnp.int32)
        indices = jnp.broadcast_to(jnp.arange(seq_length, dtype=jnp.int32)[None, :], rows.shape)
        tables = jnp.stack([rows, indices, indices - starts])
        tables = tables.reshape(3, 2, 2, 2, -1)
        tables = flip_if(near, flip_if(far, tables, 2), 3)
        tables = tables.transpose(0, 1, 3, 2, 4).reshape(3, 2, seq_length)
        inverse = rotary_base ** (-(jnp.arange(HEAD_DIM // 2, dtype=jnp.float32) * 2.0) / HEAD_DIM)
        angles = tables[2].astype(jnp.float32)[:, :, None] * inverse
        angles = jnp.concatenate([angles, angles], axis=-1)
        same_doc = tables[0][:, :, None] == tables[0][:, None, :]
        causal = tables[1][:, :, None] >= tables[1][:, None, :]
        allowed = jnp.logical_and(same_doc, causal)[:, None]
        return allowed, jnp.cos(angles)[:, None], jnp.sin(angles)[:, None]

    def body(
        hidden_in,
        segment_ids,
        query_weight,
        key_weight,
        value_weight,
        output_weight,
        gate_weight,
        up_weight,
        down_weight,
        query_gain,
        key_gain,
        attention_gain,
        feedforward_gain,
        out_grad,
    ):
        model = hidden_in.shape[1]
        seq_length = segment_ids.shape[1]
        width = query_weight.shape[1] // 2
        hidden = gate_weight.shape[1] // 2
        heads = width // HEAD_DIM
        scale_factor = HEAD_DIM ** (-0.5)

        hidden_own = to_relative(hidden_in)
        tokens_all = gather_tokens(hidden_own)
        qkv_full = gather_weight([query_weight, key_weight, value_weight])
        gains = gather_gains([query_gain, key_gain, attention_gain, feedforward_gain])
        output_full = gather_weight([output_weight.T])
        gate_up_full = gather_weight([gate_weight, up_weight])
        down_full = gather_weight([down_weight.T])

        allowed, cosine, sine = token_tables(segment_ids)
        column = (lax.axis_index(far) * 2 + lax.axis_index(near)) * 2 + lax.axis_index(pair)
        column_start = column * width
        own_gains = lax.dynamic_slice_in_dim(from_relative(gains[:2]), column_start, width, 1)
        attention_scale, feed_scale = gains[2], gains[3]

        def to_heads(values):
            return values.reshape(2, seq_length, heads, HEAD_DIM).transpose(0, 2, 1, 3)

        def from_heads(values):
            return values.transpose(0, 2, 1, 3).reshape(-1, width)

        qkv_raw = dot(tokens_all, qkv_full, 1, 0)
        query_raw, key_raw, value_raw = jnp.split(qkv_raw, 3, axis=1)
        squares = sum_group(
            jnp.stack([jnp.sum(query_raw * query_raw, axis=1), jnp.sum(key_raw * key_raw, axis=1)])
        )
        inverses = lax.rsqrt(squares / model + epsilon)
        query_inv, key_inv = inverses[0], inverses[1]

        def rotate(raw, inverse, gain):
            values = to_heads(raw * inverse[:, None] * gain)
            return narrow(values * cosine + rotate_half(values) * sine)

        query_rot = rotate(query_raw, query_inv, own_gains[0])
        key_rot = rotate(key_raw, key_inv, own_gains[1])
        value_cast = narrow(to_heads(value_raw))

        def product(former, latter, former_dim, latter_dim):
            return lax.dot_general(
                former,
                latter,
                (((former_dim,), (latter_dim,)), ((0, 1), (0, 1))),
                preferred_element_type=jnp.float32,
            )

        scores = product(query_rot, key_rot, 3, 3) * scale_factor
        log_totals = jnp.log(jnp.sum(jnp.where(allowed, jnp.exp(scores), 0.0), axis=-1))
        probs = jnp.where(allowed, jnp.exp(scores - log_totals[..., None]), 0.0)
        context = from_heads(narrow(product(narrow(probs), value_cast, 3, 2)))
        attention_sum = scatter_tokens(context, output_full)
        attention_inv = rms_inverse(attention_sum)
        residual = wide(hidden_own) + attention_sum * attention_inv[:, None] * attention_scale
        mixed_all = gather_tokens(narrow(residual))
        gate_up = dot(mixed_all, gate_up_full, 1, 0)
        gate_pre, up_pre = gate_up[:, :hidden], gate_up[:, hidden:]
        sigmoid_gate = jax.nn.sigmoid(gate_pre)
        activated = gate_pre * sigmoid_gate
        hidden_units = narrow(activated * up_pre)
        feed_sum = scatter_tokens(hidden_units, down_full)
        feed_inv = rms_inverse(feed_sum)
        hidden_out = narrow(residual + feed_sum * feed_inv[:, None] * feed_scale)

        upstream = wide(to_relative(out_grad))
        weighted = feed_scale * upstream
        feed_gain_grad = jnp.sum(upstream * feed_sum * feed_inv[:, None], axis=0)
        feed_grad = narrow(
            norm_back(feed_sum, feed_inv, weighted, jnp.mean(weighted * feed_sum, axis=1))
        )
        feed_grad_all = gather_tokens(feed_grad)
        (down_grad,) = scatter_weight(feed_grad_all, hidden_units, [hidden])
        hidden_grad = dot(feed_grad_all, down_full, 1, 0)
        gate_grad = hidden_grad * up_pre * sigmoid_gate * (1.0 + gate_pre * (1.0 - sigmoid_gate))
        up_grad = hidden_grad * activated
        gate_up_grad = jnp.concatenate([narrow(gate_grad), narrow(up_grad)], axis=1)
        gate_weight_grad, up_weight_grad = scatter_weight(mixed_all, gate_up_grad, [hidden, hidden])
        stream_grad = upstream + scatter_tokens(gate_up_grad, gate_up_full)
        attention_weighted = attention_scale * stream_grad
        attention_gain_grad = jnp.sum(stream_grad * attention_sum * attention_inv[:, None], axis=0)
        attention_grad = narrow(
            norm_back(
                attention_sum,
                attention_inv,
                attention_weighted,
                jnp.mean(attention_weighted * attention_sum, axis=1),
            )
        )
        attention_grad_all = gather_tokens(attention_grad)
        (output_grad,) = scatter_weight(attention_grad_all, context, [width])
        context_grad = to_heads(narrow(dot(attention_grad_all, output_full, 1, 0)))
        value_grad = narrow(from_heads(product(narrow(probs), context_grad, 2, 2)))
        probs_grad = product(context_grad, value_cast, 3, 3)
        row_inner = jnp.sum(probs * probs_grad, axis=-1)
        score_grad = narrow(probs * (probs_grad - row_inner[..., None]) * scale_factor)

        def rotate_back(gradient):
            return from_heads(gradient * cosine - rotate_half(gradient * sine))

        query_norm_grad = rotate_back(product(score_grad, key_rot, 3, 2))
        key_norm_grad = rotate_back(product(score_grad, query_rot, 2, 2))
        query_gain_grad = jnp.sum(query_norm_grad * query_raw * query_inv[:, None], axis=0)
        key_gain_grad = jnp.sum(key_norm_grad * key_raw * key_inv[:, None], axis=0)
        query_weighted = own_gains[0] * query_norm_grad
        key_weighted = own_gains[1] * key_norm_grad
        inner = (
            sum_group(
                jnp.stack(
                    [
                        jnp.sum(query_weighted * query_raw, axis=1),
                        jnp.sum(key_weighted * key_raw, axis=1),
                    ]
                )
            )
            / model
        )
        query_grad = narrow(norm_back(query_raw, query_inv, query_weighted, inner[0]))
        key_grad = narrow(norm_back(key_raw, key_inv, key_weighted, inner[1]))
        qkv_grad = jnp.concatenate([query_grad, key_grad, value_grad], axis=1)
        query_weight_grad, key_weight_grad, value_weight_grad = scatter_weight(
            tokens_all, qkv_grad, [width] * 3
        )
        grad_in = stream_grad + scatter_tokens(qkv_grad, qkv_full)

        zeros = jnp.zeros((2, model), jnp.float32)
        head_gains = lax.dynamic_update_slice_in_dim(
            zeros, jnp.stack([query_gain_grad, key_gain_grad]), column_start, 1
        )
        gain_grads = scatter_gains(
            jnp.concatenate(
                [to_relative(head_gains), attention_gain_grad[None], feed_gain_grad[None]], axis=0
            )
        )
        return (
            from_relative(hidden_out),
            from_relative(grad_in),
            query_weight_grad,
            key_weight_grad,
            value_weight_grad,
            output_grad.T,
            gate_weight_grad,
            up_weight_grad,
            down_grad.T,
            gain_grads[0],
            gain_grads[1],
            gain_grads[2],
            gain_grads[3],
        )

    return body


def solution(mesh):
    dp_bits = int(math.log2(mesh.shape["dp"]))
    tp_bits = int(math.log2(mesh.shape["tensor"]))
    dp = tuple(f"d{i}" for i in range(dp_bits))
    tp = tuple(f"t{i}" for i in range(tp_bits))
    split = Mesh(mesh.devices.reshape((2,) * (dp_bits + tp_bits)), dp + tp)
    both, rows, cols = P(dp + tp, None), P(dp, tp), P(tp, dp)
    vector = P(dp + tp)
    return jax.shard_map(
        make_body(dp, tp),
        mesh=split,
        in_specs=(both, P(dp, None), rows, rows, rows, cols, rows, rows, cols)
        + (vector,) * 4
        + (both,),
        out_specs=(both, both, rows, rows, rows, cols, rows, rows, cols) + (vector,) * 4,
        check_vma=False,
    )
```
